128 devices in a mesh: fsdp: 8 (over x, core), owner: 16 (over y, z).
Axes of the slice: x: 4, y: 4, z: 4, core: 2. Of those that a mesh axis runs over, the one named last changes fastest.
Arguments:
- grads: bfloat16 [32, 2560, 5120], P('owner', 'fsdp'), may hold values from -6 to 6
- assign: int32 [320, 1], replicated, may hold values from 0 to 15; in each aligned block of 20 rows (0 to 19, 20 to 39, ...) at most 2 rows name the same one
- bases: bfloat16 [16, 32, 512, 512], P('owner', None, 'fsdp'), may hold values from -0.25 to 0.25
- eigvals: bfloat16 [16, 32, 512], P('owner'), may hold values from 0.099609375 to 10
Outputs:
- update: bfloat16 [32, 2560, 5120], P('owner', 'fsdp')
The draws below stay inside these ranges and needn't reach their ends.
Inputs may be any that keep to these rules, and one draw needn't show every extreme that they name: `assign`: within each aligned block of 20 units (the matrices of one index of owner) no owner is named more than 2 times; in some block one owner is named exactly 2 times.
All inputs are finite; a program needn't handle non-finite values.
Results may differ from the reference program's by a relative error of at most 0.0043.
Values may be sent and summed in bfloat16 or wider, within the bound.
No kernel may reach another device: no remote copies, remote signals or barrier semaphores. Data moves between devices by JAX's collectives and lax.ppermute only.
A program may use at most 128 MiB of HBM per device.

```python
import math
import jax
import jax.numpy as jnp
import numpy as np
from jax import lax

C = 5120
R = 2560
BLK = 512
NBLK = 10
MATS = 32
UNITS_SRC = 20
UNITS = 320
PEER_CAP = 2
SLOTS = 32
N_OWNER = 16


def block_scale(own_key, dims, cuts, low, top_value):
    def one(dim, blocks):
        heights = jax.random.uniform(jax.random.fold_in(jax.random.fold_in(own_key, 6), dim), (blocks,), jnp.float32, low / len(cuts), top_value / len(cuts))
        return jnp.repeat(jnp.exp(heights), dims[dim] // blocks).reshape((-1,) + (1,) * (len(dims) - dim - 1))

    loudness = one(*cuts[0])
    for cut in cuts[1:]:
        loudness = loudness * one(*cut)
    return loudness


def assign_block(own_key, own, number, rows, count, top, reach, lean):
    ranking = jax.random.permutation(own_key, count)
    crowded, ordinary = shares(count, rows * top, reach, lean, True), shares(count, rows * top, reach, lean, False)
    places = jnp.arange(count)

    def named(sizes, offset_by):
        used = int((sizes > 0).sum())
        fixed = max(1, used // 4)
        shifted = fixed + (places - fixed + offset_by * (used - fixed)) % max(1, count - fixed)
        return jnp.zeros((count,), jnp.int32).at[ranking[jnp.where(places < fixed, places, shifted)]].set(jnp.asarray(sizes, jnp.int32))

    sizes = jnp.where(number % 4 == 0, named(crowded, number // 4), named(ordinary, number - number // 4 - 1))
    mixed = jax.random.permutation(jax.random.fold_in(own, 3), count)
    giver, sink = mixed[0:count // 2 * 2:2], mixed[1:count // 2 * 2:2]
    slack = jnp.minimum(sizes[giver] - 1, reach - sizes[sink]) // 2
    slack = jnp.where((giver == ranking[0]) | (sink == ranking[0]) | (sizes[sink] == 0), 0, jnp.maximum(slack, 0))
    shifted = jax.random.randint(jax.random.fold_in(own, 4), (count // 2,), 0, 1 << 20) % (slack + 1)
    sizes = sizes.at[giver].add(-shifted).at[sink].add(shifted)
    items = jnp.searchsorted(jnp.cumsum(sizes), jnp.arange(rows * top), side="right").astype(jnp.int32)
    listing = items.reshape(top, rows).T
    listing = listing[jax.random.permutation(jax.random.fold_in(own, 1), rows)]
    offset_by = jax.random.randint(jax.random.fold_in(own, 2), (rows, 1), 0, top)
    return jnp.take_along_axis(listing, (jnp.arange(top)[None, :] + offset_by) % top, axis=1)


def shares(count, total, most, slope, full):
    weights = [(1 << 20) // math.isqrt(standing ** slope) + 1 for standing in range(1, count + 1)]
    largest = most if full else min(most, max(-(-total // count), total * weights[0] // sum(weights)))
    least = 1 if total - largest >= count - 1 else 0
    holding, surplus = [largest] + [least] * (count - 1), total - largest - least * (count - 1)
    while surplus > 0:
        movable = [i for i in range(1, count) if holding[i] < largest] or [i for i in range(1, count) if holding[i] < most]
        mass, remaining = sum([weights[i] for i in movable]), surplus
        for i in movable:
            more = min(most - holding[i], max(1, remaining * weights[i] // mass), surplus)
            holding[i] = holding[i] + more
            surplus = surplus - more
    return np.array(holding)


def normal_values(own_key, extent, scale, bound, cuts=(), kind=jnp.bfloat16):
    loudness = block_scale(own_key, extent, cuts, -0.22, 0.18) if cuts else 1.0
    drawn = jax.random.normal(own_key, extent, jnp.float32) * scale * loudness
    return jnp.minimum(jnp.maximum(drawn, -bound), bound).astype(kind)


def setup_inputs(seed: int = 0) -> dict:
    key_of = jax.random.split(jax.random.key(seed), 5)
    grads = normal_values(key_of[0], (MATS, R, C), 1.0, 6.0, ((0, 16), (1, 8)))
    assign_keys = jax.random.split(jax.random.fold_in(key_of[1], 1), UNITS // UNITS_SRC)
    assign_turns = jax.random.permutation(jax.random.fold_in(key_of[1], 3), UNITS // UNITS_SRC)
    assign = jax.vmap(lambda own, number: assign_block(jax.random.fold_in(key_of[1], 2), own, number, UNITS_SRC, N_OWNER, 1, PEER_CAP, 2))(assign_keys, assign_turns).reshape((UNITS, 1))
    bases = normal_values(key_of[2], (N_OWNER, SLOTS, BLK, BLK), BLK ** -0.5, 0.25, ((0, 16), (2, 8)))
    eigvals = jnp.clip(jnp.exp(math.log(10.0) - 4.609084 * jax.random.uniform(key_of[3], (N_OWNER, SLOTS, BLK), jnp.float32) ** block_scale(key_of[3], (N_OWNER, SLOTS, BLK), ((0, 16),), -0.2, 0.2)), 0.099609375, 10.0).astype(jnp.bfloat16)
    return dict(grads=grads, assign=assign, bases=bases, eigvals=eigvals)


DAMPING = 0.1


def reference(grads, assign, bases, eigvals):
    owner_table = assign[:, 0].reshape(N_OWNER, UNITS_SRC)
    owner_ids = jnp.arange(N_OWNER, dtype=jnp.int32)
    owner_hits = (owner_table[:, :, None] == owner_ids[None, None, :]).astype(jnp.int32)
    slot_ranks = jnp.sum((jnp.cumsum(owner_hits, axis=1) - 1) * owner_hits, axis=2).astype(jnp.int32)
    sources = jnp.arange(N_OWNER, dtype=jnp.int32)[:, None] * jnp.ones((1, UNITS_SRC), jnp.int32)
    slot_ids = (sources * PEER_CAP + slot_ranks).reshape(-1).astype(jnp.int32)
    owner_flat = owner_table.reshape(-1).astype(jnp.int32)
    panels = grads.reshape(MATS, R, NBLK, BLK).transpose(0, 2, 1, 3).reshape(UNITS, R, BLK)

    def one_unit(items):
        panel_block, owner_id, slot_id = items
        basis_block = bases[owner_id, slot_id]
        eigen_vals = eigvals[owner_id, slot_id].astype(jnp.float32)
        turned = jnp.dot(panel_block, basis_block, preferred_element_type=jnp.float32)
        scaled = (turned / (eigen_vals[None, :] + DAMPING)).astype(jnp.bfloat16)
        return jnp.dot(scaled, basis_block.T, preferred_element_type=jnp.float32).astype(jnp.bfloat16)

    result = lax.map(one_unit, (panels, owner_flat, slot_ids))
    return result.reshape(MATS, NBLK, R, BLK).transpose(0, 2, 1, 3).reshape(MATS, R, C)
```

```python
import jax
import jax.numpy as jnp
from jax import lax
from jax.experimental import pallas as pl
from jax.experimental.pallas import tpu as pltpu
from jax.sharding import PartitionSpec as P

BLK = 512
DAMPING = 0.1


def rotate_kernel(grad_ref, basis_ref, eigen_ref, out_ref):
    shards, _, shard_rows, width = basis_ref.shape
    basis = basis_ref[...].reshape(shards * shard_rows, width)
    inverse = 1.0 / (eigen_ref[0].astype(jnp.float32) + DAMPING)
    turned = jnp.dot(grad_ref[0], basis, preferred_element_type=jnp.float32)
    scaled = (turned * inverse).astype(jnp.bfloat16)
    out_ref[0] = lax.dot_general(
        scaled, basis, (((1,), (1,)), ((), ())), preferred_element_type=jnp.float32
    ).astype(out_ref.dtype)


def rotate(grads, bases, eigen):
    matrices, row_count, col_count = grads.shape
    block_count = col_count // BLK
    shards, unit_count, shard_rows, width = bases.shape
    flops = 4 * unit_count * row_count * BLK * BLK
    moved = 2 * (2 * grads.size + bases.size)
    return pl.pallas_call(
        rotate_kernel,
        out_shape=jax.ShapeDtypeStruct(grads.shape, grads.dtype),
        grid=(unit_count,),
        in_specs=[
            pl.BlockSpec((1, row_count, BLK), lambda u: (u // block_count, 0, u % block_count)),
            pl.BlockSpec((shards, 1, shard_rows, width), lambda u: (0, u, 0, 0)),
            pl.BlockSpec((1, 1, BLK), lambda u: (u, 0, 0)),
        ],
        out_specs=pl.BlockSpec(
            (1, row_count, BLK), lambda u: (u // block_count, 0, u % block_count)
        ),
        cost_estimate=pl.CostEstimate(flops=flops, bytes_accessed=moved, transcendentals=0),
        name="rotate",
    )(grads, bases, eigen.reshape(unit_count, 1, BLK))


def per_device(grads, assign, bases, eigvals):
    owner_count = lax.axis_size("owner")
    owner_here = lax.axis_index("owner")
    matrices, row_count, col_count = grads.shape
    unit_count = matrices * (col_count // BLK)
    per_peer = bases.shape[1] // owner_count
    owners = lax.dynamic_slice_in_dim(assign[:, 0], owner_here * unit_count, unit_count)
    units = jnp.arange(unit_count, dtype=jnp.int32)
    same = (owners[:, None] == owners[None, :]) & (units[None, :] < units[:, None])
    slots = owners * per_peer + jnp.sum(same.astype(jnp.int32), axis=1)
    arrived = lax.all_to_all(bases[0], "owner", split_axis=0, concat_axis=0, tiled=True)
    eigen = lax.all_to_all(eigvals[0], "owner", split_axis=0, concat_axis=0, tiled=True)
    mine = arrived[slots]
    whole = lax.all_gather(mine, "fsdp", axis=0)
    return rotate(grads, whole, eigen[slots])


def solution(mesh):
    in_specs = (
        P("owner", "fsdp", None),
        P(),
        P("owner", None, "fsdp", None),
        P("owner", None, None),
    )
    out_specs = P("owner", "fsdp", None)
    return jax.shard_map(
        per_device, mesh=mesh, in_specs=in_specs, out_specs=out_specs, check_vma=False
    )
```
